32 devices in a mesh: context: 4 (over z), dp: 4 (over x, core), tensor: 2 (over y).
Axes of the slice: x: 2, y: 2, z: 4, core: 2. Of those that a mesh axis runs over, the one named last changes fastest.
Arguments:
- query_rows: bfloat16 [4, 512, 4096], P('dp', 'context', 'tensor'), may hold values from -6 to 6
- key_rows: bfloat16 [4, 512, 4096], P('dp', 'context', 'tensor'), may hold values from -6 to 6
- value_rows: bfloat16 [4, 512, 4096], P('dp', 'context', 'tensor'), may hold values from -6 to 6
- out_weight: bfloat16 [4096, 6144], P('tensor', 'dp'), may hold values from -0.125 to 0.125
- grad_out: bfloat16 [4, 512, 6144], P('dp', 'context'), may hold values from -4 to 4
Outputs:
- attended: bfloat16 [4, 512, 6144], P('dp', 'context', 'tensor')
- grad_query: bfloat16 [4, 512, 4096], P('dp', 'context', 'tensor')
- grad_key: bfloat16 [4, 512, 4096], P('dp', 'context', 'tensor')
- grad_value: bfloat16 [4, 512, 4096], P('dp', 'context', 'tensor')
The draws below stay inside these ranges and needn't reach their ends.
All inputs are finite; a program needn't handle non-finite values.
Results may differ from the reference program's by a relative error of at most 0.025.
Values may be sent and summed in bfloat16 or wider, within the bound.
No kernel may reach another device: no remote copies, remote signals or barrier semaphores. Data moves between devices by JAX's collectives and lax.ppermute only.
A program may use at most 128 MiB of HBM per device.

```python
import jax
import jax.numpy as jnp
from jax import lax

D = 6144
DH = 128
HEADS = 32
TOK_DEV = 128
HD = 4096
LENGTH = 512
SEQS = 4
N_CONTEXT = 4
N_TENSOR = 2


def strengthened(values, stream_key, source, target, blocks, factor):
    def block_of(position):
        return (jnp.arange(values.shape[position]) // (values.shape[position] // blocks)).reshape((-1,) + (1,) * (values.ndim - 1 - position))

    one_side = jax.random.permutation(stream_key, blocks)[block_of(target)]
    other_side = (block_of(target) + blocks // 2) % blocks
    return jnp.where((block_of(source) == one_side) | (block_of(source) == other_side), factor * values, values)


def shard_levels(stream_key, dims, cuts, low, top_value):
    factor_of = 1.0
    for axis_at, parts in cuts:
        steps = jax.random.uniform(jax.random.fold_in(jax.random.fold_in(stream_key, 6), axis_at), (parts,), jnp.float32, low / len(cuts), top_value / len(cuts))
        factor_of = factor_of * jnp.repeat(jnp.exp(steps), dims[axis_at] // parts).reshape((-1,) + (1,) * (len(dims) - 1 - axis_at))
    return factor_of


def normal_values(own_key, dims, width, bound, cuts=(), dtype=jnp.bfloat16):
    values = jax.random.normal(own_key, dims, jnp.float32) * width
    if len(cuts) > 0:
        values = shard_levels(own_key, dims, cuts, -0.22, 0.18) * values
    return jnp.clip(values, min=-bound, max=bound).astype(dtype)


def heavy_noise(rng, extent, width, bound, cuts, heavy, dtype=jnp.bfloat16):
    drawn = width * jax.random.normal(rng, extent, jnp.float32)
    if cuts:
        drawn = drawn * shard_levels(rng, extent, cuts, -0.22, 0.18)
    return jnp.clip(strengthened(drawn, jax.random.fold_in(rng, 3), *heavy), -bound, bound).astype(dtype)


def setup_inputs(seed: int = 0) -> dict:
    key_list = jax.random.split(jax.random.key(seed), 6)
    query_rows = normal_values(key_list[0], (SEQS, LENGTH, HD), 1.0, 6.0, ((0, 4), (1, 4), (2, 2)))
    key_rows = normal_values(key_list[1], (SEQS, LENGTH, HD), 1.0, 6.0, ((0, 4), (1, 4), (2, 2)))
    value_rows = normal_values(key_list[2], (SEQS, LENGTH, HD), 1.0, 6.0, ((0, 4), (1, 4), (2, 2)))
    out_weight = heavy_noise(key_list[3], (HD, D), HD ** -0.5, 0.125, ((0, 2), (1, 4)), (0, 1, 4, 2.0))
    grad_out = normal_values(key_list[4], (SEQS, LENGTH, D), 0.5, 4.0, ((0, 4), (1, 4)))
    return dict(query_rows=query_rows, key_rows=key_rows, value_rows=value_rows, out_weight=out_weight, grad_out=grad_out)


def causal_tri(size):
    places = jnp.arange(size)
    return (places[:, None] >= places[None, :]).astype(jnp.float32)


def one_sequence(query_f, key_f, value_f, grad_f):
    factor = (DH * LENGTH) ** -0.5
    precise = lax.Precision.HIGHEST
    causal = causal_tri(TOK_DEV)

    def blocks(array):
        return array.reshape(N_CONTEXT, TOK_DEV, HEADS, DH)

    q_all, k_all, v_all, g_all = blocks(query_f), blocks(key_f), blocks(value_f), blocks(grad_f)

    def forward_step(state, pieces):
        q_blk, k_blk, v_blk, g_blk = pieces
        scores = jnp.einsum('bhd,chd->hbc', q_blk, k_blk, precision=precise) * causal
        attn_out = factor * (jnp.einsum('hbc,che->bhe', scores, v_blk, precision=precise)
                             + jnp.einsum('bhd,hde->bhe', q_blk, state, precision=precise))
        d_scores = jnp.einsum('bhe,che->hbc', g_blk, v_blk, precision=precise) * causal
        grad_q = factor * (jnp.einsum('hbc,chd->bhd', d_scores, k_blk, precision=precise)
                           + jnp.einsum('bhe,hde->bhd', g_blk, state, precision=precise))
        state = state + jnp.einsum('chd,che->hde', k_blk, v_blk, precision=precise)
        return state, (attn_out, grad_q)

    def backward_step(state, pieces):
        q_blk, k_blk, v_blk, g_blk = pieces
        scores = jnp.einsum('bhd,chd->hbc', q_blk, k_blk, precision=precise) * causal
        d_scores = jnp.einsum('bhe,che->hbc', g_blk, v_blk, precision=precise) * causal
        state = state + jnp.einsum('bhd,bhe->hde', q_blk, g_blk, precision=precise)
        grad_k = factor * (jnp.einsum('hbc,bhd->chd', d_scores, q_blk, precision=precise)
                           + jnp.einsum('che,hde->chd', v_blk, state - jnp.einsum('bhd,bhe->hde', q_blk, g_blk, precision=precise), precision=precise))
        grad_v = factor * (jnp.einsum('hbc,bhe->che', scores, g_blk, precision=precise)
                           + jnp.einsum('chd,hde->che', k_blk, state - jnp.einsum('bhd,bhe->hde', q_blk, g_blk, precision=precise), precision=precise))
        return state, (grad_k, grad_v)

    start_state = jnp.zeros((HEADS, DH, DH), jnp.float32)
    _, (attn_out, grad_q) = lax.scan(forward_step, start_state, (q_all, k_all, v_all, g_all))
    _, (grad_k, grad_v) = lax.scan(backward_step, start_state, (q_all, k_all, v_all, g_all), reverse=True)
    flat = lambda array: array.reshape(LENGTH, HD)
    return flat(attn_out), flat(grad_q), flat(grad_k), flat(grad_v)


def reference(query_rows, key_rows, value_rows, out_weight, grad_out):
    grad_attn = jnp.dot(grad_out.reshape(SEQS * LENGTH, D), out_weight.T,
                        preferred_element_type=jnp.float32).astype(jnp.bfloat16)
    grad_attn = grad_attn.reshape(SEQS, LENGTH, HD)
    attn_out, grad_q, grad_k, grad_v = jax.vmap(one_sequence)(
        query_rows.astype(jnp.float32), key_rows.astype(jnp.float32),
        value_rows.astype(jnp.float32), grad_attn.astype(jnp.float32))
    attn_flat = attn_out.astype(jnp.bfloat16).reshape(SEQS * LENGTH, HD)
    group_width = HD // N_TENSOR
    attended = jnp.zeros((SEQS * LENGTH, D), jnp.float32)
    for group in range(N_TENSOR):
        partial_out = jnp.dot(attn_flat[:, group * group_width:(group + 1) * group_width],
                              out_weight[group * group_width:(group + 1) * group_width],
                              preferred_element_type=jnp.float32)
        attended = attended + partial_out.astype(jnp.bfloat16).astype(jnp.float32)
    attended = attended.astype(jnp.bfloat16).reshape(SEQS, LENGTH, D)
    return (attended, grad_q.astype(jnp.bfloat16), grad_k.astype(jnp.bfloat16), grad_v.astype(jnp.bfloat16))
```

```python
import functools

import jax
import jax.numpy as jnp
from jax import lax
from jax.experimental import pallas as pl
from jax.experimental.pallas import tpu as pltpu
from jax.sharding import PartitionSpec as P

DH = 128
CHUNKS = 2
VMEM_LIMIT = 24 << 20

NN = (((1,), (0,)), ((), ()))
NT = (((1,), (1,)), ((), ()))
TN = (((0,), (0,)), ((), ()))


def dot(a, b, dims):
    return lax.dot_general(a, b, dims, preferred_element_type=jnp.float32)


def causal(rows):
    down = lax.broadcasted_iota(jnp.int32, (rows, rows), 0)
    across = lax.broadcasted_iota(jnp.int32, (rows, rows), 1)
    return down >= across


def head(ref, h):
    return ref[:, h * DH : (h + 1) * DH]


def call(body, name, out_shape, in_specs, out_specs, flops, nbytes, grid=(1,), scratch=(), aliases=None, prefetch=0):
    return pl.pallas_call(
        body,
        name=name,
        out_shape=out_shape,
        grid_spec=pltpu.PrefetchScalarGridSpec(
            num_scalar_prefetch=prefetch,
            grid=grid,
            in_specs=in_specs,
            out_specs=out_specs,
            scratch_shapes=list(scratch),
        ),
        input_output_aliases=aliases or {},
        compiler_params=pltpu.CompilerParams(vmem_limit_bytes=VMEM_LIMIT),
        cost_estimate=pl.CostEstimate(flops=flops, bytes_accessed=nbytes, transcendentals=0),
    )


def columns(rows, width, j):
    return pl.BlockSpec((rows, width), lambda i, *_: (0, j))


def whole(*shape):
    return pl.BlockSpec(shape, lambda i, *_: (0,) * len(shape))


def key_value_states(k, v, j, width):
    rows, heads = k.shape[0], width // DH

    def body(k_ref, v_ref, s_ref):
        for h in range(heads):
            s_ref[h * DH : (h + 1) * DH, :] = dot(head(k_ref, h), head(v_ref, h), TN).astype(jnp.bfloat16)

    return call(
        body,
        "kv_states",
        jax.ShapeDtypeStruct((width, DH), jnp.bfloat16),
        [columns(rows, width, j)] * 2,
        whole(width, DH),
        2 * rows * width * DH,
        6 * rows * width,
    )(k, v)


def attention(q, k, v, prefix, j, width, factor):
    rows, heads = q.shape[0], width // DH

    def body(q_ref, k_ref, v_ref, p_ref, o_ref):
        mask = causal(rows)
        for h in range(heads):
            qh, kh, vh = head(q_ref, h), head(k_ref, h), head(v_ref, h)
            scores = jnp.where(mask, dot(qh, kh, NT), 0.0).astype(jnp.bfloat16)
            out = dot(scores, vh, NN) + dot(qh, p_ref[h * DH : (h + 1) * DH, :], NN)
            o_ref[:, h * DH : (h + 1) * DH] = (factor * out).astype(jnp.bfloat16)

    return call(
        body,
        "attention",
        jax.ShapeDtypeStruct((rows, width), jnp.bfloat16),
        [columns(rows, width, j)] * 3 + [whole(width, DH)],
        whole(rows, width),
        6 * rows * width * DH,
        10 * rows * width,
    )(q, k, v, prefix)


def query_gradient_states(q, kept, arrived, j, width):
    rows, heads = q.shape[0], width // DH

    def body(q_ref, a_ref, b_ref, g_ref, n_ref):
        g = (a_ref[...].astype(jnp.float32) + b_ref[...].astype(jnp.float32)).astype(jnp.bfloat16)
        g_ref[...] = g
        for h in range(heads):
            n_ref[h * DH : (h + 1) * DH, :] = dot(head(q_ref, h), g[:, h * DH : (h + 1) * DH], TN).astype(jnp.bfloat16)

    return call(
        body,
        "qg_states",
        (jax.ShapeDtypeStruct((rows, width), jnp.bfloat16), jax.ShapeDtypeStruct((width, DH), jnp.bfloat16)),
        [columns(rows, width, j), whole(rows, width), whole(rows, width)],
        (whole(rows, width), whole(width, DH)),
        2 * rows * width * DH,
        10 * rows * width,
    )(q, kept, arrived)


def inside_gradients(q, k, v, g, prefix, j, width, factor):
    rows, heads = q.shape[0], width // DH

    def body(q_ref, k_ref, v_ref, g_ref, p_ref, gq_ref, gk_ref, gv_ref):
        mask = causal(rows)
        for h in range(heads):
            cut = slice(h * DH, (h + 1) * DH)
            qh, kh, vh, gh = head(q_ref, h), head(k_ref, h), head(v_ref, h), head(g_ref, h)
            scores = jnp.where(mask, dot(qh, kh, NT), 0.0).astype(jnp.bfloat16)
            d_scores = jnp.where(mask, dot(gh, vh, NT), 0.0).astype(jnp.bfloat16)
            gq = dot(d_scores, kh, NN) + dot(gh, p_ref[cut, :], NT)
            gq_ref[:, cut] = (factor * gq).astype(jnp.bfloat16)
            gk_ref[:, cut] = dot(d_scores, qh, TN)
            gv_ref[:, cut] = dot(scores, gh, TN)

    return call(
        body,
        "inside_gradients",
        (
            jax.ShapeDtypeStruct((rows, width), jnp.bfloat16),
            jax.ShapeDtypeStruct((rows, width), jnp.float32),
            jax.ShapeDtypeStruct((rows, width), jnp.float32),
        ),
        [columns(rows, width, j)] * 3 + [whole(rows, width), whole(width, DH)],
        (whole(rows, width),) * 3,
        12 * rows * width * DH,
        20 * rows * width,
    )(q, k, v, g, prefix)


def across_gradients(k, v, suffix, gk, gv, j, width, factor):
    rows, heads = k.shape[0], width // DH

    def body(k_ref, v_ref, n_ref, gk_ref, gv_ref, ok_ref, ov_ref):
        for h in range(heads):
            cut = slice(h * DH, (h + 1) * DH)
            state = n_ref[cut, :]
            ok_ref[:, cut] = (factor * (gk_ref[:, cut] + dot(head(v_ref, h), state, NT))).astype(jnp.bfloat16)
            ov_ref[:, cut] = (factor * (gv_ref[:, cut] + dot(head(k_ref, h), state, NN))).astype(jnp.bfloat16)

    return call(
        body,
        "across_gradients",
        (jax.ShapeDtypeStruct((rows, width), jnp.bfloat16),) * 2,
        [columns(rows, width, j)] * 2 + [whole(width, DH)] + [whole(rows, width)] * 2,
        (whole(rows, width),) * 2,
        4 * rows * width * DH,
        18 * rows * width,
    )(k, v, suffix, gk, gv)


def gradient_products(lefts, weight, chunk):
    rows, depth = lefts[0].shape
    width = weight.shape[0]
    count, pieces = len(lefts), width // chunk
    tile = min(512, chunk)
    per = chunk // tile

    def body(*refs):
        w_ref = refs[count]
        outs = refs[count + 1 : count + 1 + count * pieces]
        stacked = refs[-1]
        step = pl.program_id(0)

        @pl.when(step == 0)
        def _():
            for n in range(count):
                stacked[n * rows : (n + 1) * rows, :] = refs[n][...]

        product = dot(stacked[...], w_ref[...], NT).astype(jnp.bfloat16)
        for n in range(count):
            for piece in range(pieces):

                @pl.when(step // per == piece)
                def _(n=n, piece=piece):
                    at = pl.multiple_of((step % per) * tile, tile)
                    outs[n * pieces + piece][:, pl.ds(at, tile)] = product[n * rows : (n + 1) * rows]

    return call(
        body,
        "gradient_products",
        (jax.ShapeDtypeStruct((rows, chunk), jnp.bfloat16),) * (count * pieces),
        [whole(rows, depth)] * count + [pl.BlockSpec((tile, depth), lambda i: (i, 0))],
        (whole(rows, chunk),) * (count * pieces),
        2 * count * rows * depth * width,
        2 * depth * width,
        grid=(width // tile,),
        scratch=[pltpu.VMEM((count * rows, depth), jnp.bfloat16)],
    )(*lefts, weight)


def output_products(order, lefts, weight):
    count, pieces = len(lefts), len(lefts[0])
    rows, chunk = lefts[0][0].shape
    depth, width = weight.shape
    tile = 512 if width % 512 == 0 else 128

    def body(order_ref, *refs):
        w_ref = refs[count * pieces]
        outs = refs[count * pieces + 1 : count * pieces + 1 + count]
        stacked = refs[-1]
        step = pl.program_id(0)

        @pl.when(step == 0)
        def _():
            for i in range(count):
                for n in range(count):

                    @pl.when(order_ref[i] == n)
                    def _(i=i, n=n):
                        for p in range(pieces):
                            stacked[i * rows : (i + 1) * rows, p * chunk : (p + 1) * chunk] = refs[n * pieces + p][...]

        product = dot(stacked[...], w_ref[...], NN).astype(jnp.bfloat16)
        for i in range(count):
            outs[i][...] = product[i * rows : (i + 1) * rows]

    return call(
        body,
        "output_products",
        (jax.ShapeDtypeStruct((rows, width), jnp.bfloat16),) * count,
        [whole(rows, chunk)] * (count * pieces) + [pl.BlockSpec((depth, tile), lambda i, o: (0, i))],
        (pl.BlockSpec((rows, tile), lambda i, o: (0, i)),) * count,
        2 * count * rows * depth * width,
        2 * depth * width,
        grid=(width // tile,),
        scratch=[pltpu.VMEM((count * rows, depth), jnp.bfloat16)],
        prefetch=1,
    )(order, *[piece for left in lefts for piece in left], weight)


def exchange(array, axis, mask):
    return lax.ppermute(array, axis, [(i, i ^ mask) for i in range(lax.axis_size(axis))])


def running_sums(states, axis, reverse):
    devices = lax.axis_size(axis)
    links = [(i, i + 1) for i in range(devices - 1)]
    if reverse:
        links = [(devices - 1 - a, devices - 1 - b) for a, b in links]
    sums = [None] * len(states)
    arrived = {}
    for stage in range(len(links) + len(states) - 1):
        for j in range(len(states)):
            link = stage - j
            if 0 <= link < len(links):
                send = states[j] if sums[j] is None else states[j] + sums[j]
                arrived[j] = lax.ppermute(send, axis, [links[link]])
        for j in range(len(states)):
            if 0 <= stage - j < len(links):
                sums[j] = arrived[j] if sums[j] is None else sums[j] + arrived[j]
    return sums


def shards(query_rows, key_rows, value_rows, out_weight, grad_out):
    seq_rows, head_width = query_rows.shape[1:]
    n_dp, n_tensor = lax.axis_size("dp"), lax.axis_size("tensor")
    me, my_group = lax.axis_index("dp"), lax.axis_index("tensor")
    factor = float(DH * seq_rows * lax.axis_size("context")) ** (-0.5)
    piece = out_weight.shape[1]
    chunks = CHUNKS if head_width % (CHUNKS * DH) == 0 else 1
    width = head_width // chunks
    q, k, v = query_rows[0], key_rows[0], value_rows[0]
    masks = range(1, n_dp)
    bits = [1 << b for b in range(n_dp.bit_length() - 1)]

    def columns_for(mask):
        return lax.dynamic_slice(grad_out[0], (0, (me ^ mask) * piece), (seq_rows, piece))

    taken = {0: columns_for(0)}
    for mask in reversed(masks):
        taken[mask] = exchange(columns_for(mask), "dp", mask)

    local_kv = [key_value_states(k, v, j, width) for j in range(chunks)]
    prefix = running_sums(local_kv, "context", False)

    partial = {}
    top = bits[-1]
    for group in ([m for m in range(n_dp) if m < top], [m for m in range(n_dp) if m >= top]):
        products = gradient_products([taken[m] for m in group], out_weight, width)
        for at, mask in enumerate(group):
            partial[mask] = products[at * chunks : (at + 1) * chunks]

    def summed(j):
        held = {mask: partial[mask][j] for mask in range(n_dp)}
        for bit in bits[:-1]:
            landed = {mask ^ bit: exchange(held[mask], "dp", bit) for mask in held if mask & bit}
            held = {mask: held[mask] + landed[mask] for mask in landed}
        return held[0], exchange(held[top], "dp", top)

    attn = [attention(q, k, v, prefix[j], j, width, factor) for j in range(chunks)]
    grad, local_qg = [], []
    for j in range(chunks):
        kept, arrived = summed(j)
        g, states = query_gradient_states(q, kept, arrived, j, width)
        grad.append(g)
        local_qg.append(states)
    suffix = running_sums(local_qg, "context", True)

    gathered = {0: attn}
    for bit in reversed(bits):
        for mask in list(gathered):
            gathered[mask ^ bit] = [exchange(part, "dp", bit) for part in gathered[mask]]

    fine = max(n_dp // n_tensor, 1)
    coarse = max(n_tensor // n_dp, 1)
    base = (my_group // coarse) * fine + me % fine
    order = jnp.stack([base ^ i ^ me for i in range(n_dp)]).astype(jnp.int32)
    products = output_products(order, [gathered[m] for m in range(n_dp)], out_weight)
    part_width = piece // coarse
    landed = []
    for i in range(n_dp):
        for c in range(coarse):
            pairs = []
            for d in range(n_dp):
                for t in range(n_tensor):
                    s = ((t // coarse) * fine + d % fine) ^ i
                    to = (d // fine) * coarse + ((t % coarse) ^ c)
                    pairs.append((d * n_tensor + t, s * n_tensor + to))
            block = products[i]
            if coarse > 1:
                at = ((my_group % coarse) ^ c) * part_width
                block = lax.dynamic_slice(block, (0, at), (seq_rows, part_width))
            landed.append(lax.ppermute(block, ("dp", "tensor"), pairs))
    order_in = [sum(landed[i * coarse + c].astype(jnp.float32) for i in range(n_dp) if i % fine == f for c in range(coarse)) for f in range(fine)]
    order_in = [part.astype(jnp.bfloat16) for part in order_in]
    attended = jnp.zeros((seq_rows, fine * part_width), jnp.bfloat16)
    for f in range(fine):
        attended = lax.dynamic_update_slice(attended, order_in[f], (0, ((me % fine) ^ f) * part_width))

    grads = [[], [], []]
    for j in range(chunks):
        gq, gk, gv = inside_gradients(q, k, v, grad[j], prefix[j], j, width, factor)
        gk, gv = across_gradients(k, v, suffix[j], gk, gv, j, width, factor)
        for into, part in zip(grads, (gq, gk, gv)):
            into.append(part)
    gq, gk, gv = (jnp.concatenate(parts, axis=1)[None] for parts in grads)
    return attended[None], gq, gk, gv


def solution(mesh):
    rows = P("dp", "context", "tensor")
    in_specs = (rows, rows, rows, P("tensor", "dp"), P("dp", "context", None))
    return jax.shard_map(shards, mesh=mesh, in_specs=in_specs, out_specs=(rows,) * 4, check_vma=False)
```

```python
import jax
import jax.numpy as jnp
from jax import lax
from jax.experimental import pallas as pl
from jax.experimental.pallas import tpu as pltpu
from jax.sharding import PartitionSpec as P


DH = 128
VMEM_LIMIT = 16 << 20
FAR_FIRST_SHARE = 0.5

NN = (((1,), (0,)), ((), ()))
NT = (((1,), (1,)), ((), ()))
TN = (((0,), (0,)), ((), ()))


def dot(a, b, dims):
    return lax.dot_general(a, b, dims, preferred_element_type=jnp.float32)


def causal(rows):
    down = lax.broadcasted_iota(jnp.int32, (rows, rows), 0)
    across = lax.broadcasted_iota(jnp.int32, (rows, rows), 1)
    return down >= across


def heads_in(width):
    return [slice(h * DH, (h + 1) * DH) for h in range(width // DH)]


def bf16(*shape):
    return jax.ShapeDtypeStruct(shape, jnp.bfloat16)


def f32(*shape):
    return jax.ShapeDtypeStruct(shape, jnp.float32)


class Stays:
    def __init__(self, array):
        self.array = pltpu.with_memory_space_constraint(array, pltpu.HBM)


class Layout:
    def __init__(self, heads_here):
        self.n_dp, self.n_tensor, self.n_context = (lax.axis_size(axis) for axis in ("dp", "tensor", "context"))
        self.owned = self.n_context & (self.n_context - 1) == 0 and heads_here % self.n_context == 0 and self.n_context > 1
        self.parts = self.n_context if self.owned else 2 if heads_here % 2 == 0 else 1
        self.width = heads_here // self.parts * DH
        self.fine, self.coarse = max(self.n_dp // self.n_tensor, 1), max(self.n_tensor // self.n_dp, 1)

        self.halved = self.fine == 2 and self.n_tensor == 2

    def part(self, m):
        return lax.axis_index("context") ^ m if self.owned else m

    def columns(self, m, offset=0, size=None):
        start = self.part(m) * self.width + offset
        if self.owned:
            start = pl.multiple_of(start, DH)
        return pl.ds(start, self.width if size is None else size)

    def swap(self):
        me, group = lax.axis_index("dp"), lax.axis_index("tensor")
        return ((group // self.coarse) * self.fine + me % self.fine) ^ me

    def place(self, f):
        return (lax.axis_index("dp") ^ f) % self.fine


def call(body, out_shape, operands, flops, nbytes, scratch=(), away=0, aliases=None):
    return pl.pallas_call(
        body,
        out_shape=out_shape,
        in_specs=[pl.BlockSpec(memory_space=pl.ANY if isinstance(x, Stays) else pltpu.VMEM) for x in operands],
        out_specs=tuple(pl.BlockSpec(memory_space=pltpu.HBM if n < away else pltpu.VMEM) for n in range(len(out_shape)))
        if isinstance(out_shape, tuple)
        else pl.BlockSpec(memory_space=pltpu.HBM if away else pltpu.VMEM),
        input_output_aliases=aliases or {},
        scratch_shapes=list(scratch),
        compiler_params=pltpu.CompilerParams(vmem_limit_bytes=VMEM_LIMIT),
        cost_estimate=pl.CostEstimate(flops=flops, bytes_accessed=nbytes, transcendentals=0),
    )(*[x.array if isinstance(x, Stays) else x for x in operands])


def column_blocks(layout, grad_out, masks, halves):
    rows, total = grad_out.shape
    piece = total // layout.n_dp
    heights = [rows // layout.n_tensor if mask in halves else rows for mask in masks]

    def body(g_ref, *refs):
        outs, sems = refs[:-1], refs[-1]
        copies = []
        for n, mask in enumerate(masks):
            start = pl.multiple_of((lax.axis_index("dp") ^ mask) * piece, DH)
            top = pl.multiple_of(lax.axis_index("tensor") * heights[n], 16) if mask in halves else 0
            source = g_ref.at[pl.ds(top, heights[n]), pl.ds(start, piece)]
            copies.append(pltpu.make_async_copy(source, outs[n], sems.at[n]))
            copies[-1].start()
        for copy in copies:
            copy.wait()

    shapes = tuple(bf16(height, piece) for height in heights)
    scratch = [pltpu.SemaphoreType.DMA((len(masks),))]
    return call(body, shapes, (Stays(grad_out),), 0, 4 * piece * sum(heights), scratch=scratch)


class Sums:
    def __init__(self, first, n, arrays, reverse):
        self.first, self.n, self.arrays, self.reverse = first, n, arrays, reverse

    def read(self, refs, h):
        at = h - self.first
        rows = slice(at * DH, (at + 1) * DH)
        if len(refs) == 1:
            return refs[0][rows, :]
        place = lax.axis_index("context")
        half = self.n // 2
        there = slice(at % half * DH, (at % half + 1) * DH)
        wanted = 0 if self.reverse else 1
        mine, other = (ref[there, :].astype(jnp.float32) for ref in refs[1:])
        across = jnp.where(place % 2 == at // half, mine, other)
        total = jnp.where(place % 2 == wanted, refs[0][rows, :].astype(jnp.float32), 0.0)
        return (total + jnp.where(place // 2 == wanted, across, 0.0)).astype(jnp.bfloat16)


class Listed:
    def __init__(self, layout, arrays):
        self.layout, self.arrays = layout, arrays
        self.first, self.n = 0, len(arrays) * layout.width // DH

    def read(self, refs, h):
        part, at = divmod(h * DH, self.layout.width)
        rows = slice(at, at + DH)
        if not self.layout.owned:
            return refs[part][rows, :]
        chosen = refs[0][rows, :]
        for m in range(1, len(refs)):
            chosen = jnp.where(self.layout.part(m) == part, refs[m][rows, :], chosen)
        return chosen


def arrays_of(all_sums):
    return [array for sums in all_sums for array in sums.arrays]


def state_of(all_sums, refs, h):
    at = 0
    for sums in all_sums:
        if sums.first <= h < sums.first + sums.n:
            return sums.read(refs[at : at + len(sums.arrays)], h)
        at += len(sums.arrays)


def cuts_of(span):
    first, last = span
    return [(c // DH, slice(c, c + DH), slice(c - first, c - first + DH)) for c in range(first, last, DH)]


def key_value_states(layout, k, v):
    size = k.shape[0] * k.shape[1]

    def body(k_hbm, v_hbm, *refs):
        outs, (k_ref, v_ref, sems) = refs[:-3], refs[-3:]
        copies = [pltpu.make_async_copy(k_hbm, k_ref, sems.at[0]), pltpu.make_async_copy(v_hbm, v_ref, sems.at[1])]
        for copy in copies:
            copy.start()
        for copy in copies:
            copy.wait()
        for m in range(layout.parts):
            for cut in heads_in(layout.width):
                here = layout.columns(m, cut.start, DH)
                outs[m][cut, :] = dot(k_ref[:, here], v_ref[:, here], TN).astype(jnp.bfloat16)

    scratch = [pltpu.VMEM(k.shape, k.dtype), pltpu.VMEM(v.shape, v.dtype), pltpu.SemaphoreType.DMA((2,))]
    shapes = (bf16(layout.width, DH),) * layout.parts
    return call(body, shapes, (Stays(k), Stays(v)), 2 * size * DH, 6 * size, scratch=scratch)


def owner_sums(layout, blocks, reverse):
    count = len(blocks)
    shape = blocks[0].shape

    def body(*refs):
        held = [refs[m][...].astype(jnp.float32) for m in range(count)]
        for m in range(count):
            to = layout.part(m)
            total = jnp.zeros_like(held[0])
            for n in range(count):
                source = layout.part(n)
                taken = source > to if reverse else source < to
                total += jnp.where(taken, held[n], 0.0)
            refs[count + m][...] = total.astype(jnp.bfloat16)

    size = shape[0] * shape[1] * count
    return call(body, (bf16(*shape),) * count, tuple(blocks), size * count, 4 * size)


def pair_half(states, arrived):
    rows = states.shape[0] // 2

    def body(a_ref, b_ref, o_ref):
        odd = lax.axis_index("context") % 2 == 1
        totals = []
        for cut in (slice(0, rows), slice(rows, 2 * rows)):
            totals.append(a_ref[cut, :].astype(jnp.float32) + b_ref[cut, :].astype(jnp.float32))
        o_ref[...] = jnp.where(odd, totals[1], totals[0]).astype(jnp.bfloat16)

    return call(body, bf16(rows, DH), (states, arrived), 2 * rows * DH, 10 * rows * DH)


def attention(layout, q, k, v, prefix, first, factor):
    rows, count, width = q.shape[0], len(prefix), layout.width

    def body(q_ref, k_ref, v_ref, *refs):
        mask = causal(rows)
        for i in range(count):
            for cut in heads_in(width):
                here = layout.columns(first + i, cut.start, DH)
                qh, kh, vh = q_ref[:, here], k_ref[:, here], v_ref[:, here]
                scores = jnp.where(mask, dot(qh, kh, NT), 0.0).astype(jnp.bfloat16)
                out = dot(scores, vh, NN) + dot(qh, refs[i][cut, :], NN)
                refs[-1][:, i * width + cut.start : i * width + cut.stop] = (factor * out).astype(jnp.bfloat16)

    size = rows * width * count
    return call(body, bf16(rows, width * count), (q, k, v, *prefix), 6 * size * DH, 10 * size)


def query_gradient_states(q, kept, arrived, span):
    rows, width = q.shape[0], span[1] - span[0]

    def body(q_ref, b_ref, *refs):
        kept_refs, g_ref, n_ref = refs[:-2], refs[-2], refs[-1]
        for _, here, there in cuts_of(span):
            g = sum((ref[:, here].astype(jnp.float32) for ref in kept_refs), b_ref[:, there].astype(jnp.float32))
            g = g.astype(jnp.bfloat16)
            g_ref[:, there] = g
            n_ref[there, :] = dot(q_ref[:, here], g, TN).astype(jnp.bfloat16)

    size = rows * width
    return call(body, (bf16(rows, width), bf16(width, DH)), (q, arrived, *kept), 2 * size * DH, 10 * size)


def inside_gradients(q, k, v, g, span):
    rows, width = q.shape[0], span[1] - span[0]

    def body(q_ref, k_ref, v_ref, g_ref, gq_ref, gk_ref, gv_ref):
        mask = causal(rows)
        for _, here, there in cuts_of(span):
            qh, kh, vh, gh = q_ref[:, here], k_ref[:, here], v_ref[:, here], g_ref[:, there]
            scores = jnp.where(mask, dot(qh, kh, NT), 0.0).astype(jnp.bfloat16)
            d_scores = jnp.where(mask, dot(gh, vh, NT), 0.0).astype(jnp.bfloat16)
            gq_ref[:, there] = dot(d_scores, kh, NN)
            gk_ref[:, there] = dot(d_scores, qh, TN)
            gv_ref[:, there] = dot(scores, gh, TN)

    size = rows * width
    return call(body, (f32(rows, width),) * 3, (q, k, v, g), 10 * size * DH, 20 * size)


def query_gradients(grads, inside, prefix, spans, factor):
    rows, total, count = grads[0].shape[0], spans[-1][1], len(spans)

    def body(*refs):
        out_hbm, out_ref, sems = refs[-3:]
        copies = []
        for j, span in enumerate(spans):
            for h, here, there in cuts_of(span):
                across = dot(refs[j][:, there], state_of(prefix, refs[2 * count : -3], h), NT)
                out_ref[:, here] = (factor * (refs[count + j][:, there] + across)).astype(jnp.bfloat16)
            cut = pl.ds(span[0], span[1] - span[0])
            copies.append(pltpu.make_async_copy(out_ref.at[:, cut], out_hbm.at[:, cut], sems.at[j]))
            copies[-1].start()
        for copy in copies:
            copy.wait()

    size = rows * total
    operands = (*grads, *inside, *arrays_of(prefix))
    scratch = [pltpu.VMEM((rows, total), jnp.bfloat16), pltpu.SemaphoreType.DMA((count,))]
    return call(body, bf16(rows, total), operands, 2 * size * DH, 10 * size, scratch, 1)


def across_gradients(k, v, suffix, gk, gv, into, span, factor):
    rows, width = k.shape[0], span[1] - span[0]
    held = [] if into is None else [Stays(x) for x in into]

    def body(k_ref, v_ref, gk_ref, gv_ref, *refs):
        ok_hbm, ov_hbm, ok_ref, ov_ref, sems = refs[-5:]
        copies = []
        half = (cuts_of(span)[-1][0] + 1 + span[0] // DH) // 2
        for h, here, there in cuts_of(span):
            state = state_of(suffix, refs[len(held) : -5], h)
            ok_ref[:, there] = (factor * (gk_ref[:, there] + dot(v_ref[:, here], state, NT))).astype(jnp.bfloat16)
            ov_ref[:, there] = (factor * (gv_ref[:, there] + dot(k_ref[:, here], state, NN))).astype(jnp.bfloat16)
            if h == half - 1 or here.stop == span[1]:
                start = 0 if h == half - 1 else half * DH - span[0]
                for ref, hbm in ((ok_ref, ok_hbm), (ov_ref, ov_hbm)):
                    part = ref.at[:, pl.ds(start, there.stop - start)]
                    there_out = hbm.at[:, pl.ds(span[0] + start, there.stop - start)]
                    copies.append(pltpu.make_async_copy(part, there_out, sems.at[len(copies)]))
                    copies[-1].start()
        for copy in copies:
            copy.wait()

    size = rows * width
    operands = (k, v, gk, gv, *held, *arrays_of(suffix))
    scratch = [pltpu.VMEM((rows, width), jnp.bfloat16)] * 2 + [pltpu.SemaphoreType.DMA((4,))]
    aliases = {4: 0, 5: 1} if held else None
    return call(body, (bf16(*k.shape),) * 2, operands, 4 * size * DH, 18 * size, scratch, 2, aliases)


def first_products(grad_out, lefts, weight):
    rows = grad_out.shape[0]
    total, depth = weight.shape
    count = 1 + len(lefts)
    pieces = 4 if total % (4 * DH) == 0 else 1
    height = total // pieces

    def body(g_ref, w_ref, *refs):
        left_refs, outs, w_out = refs[: len(lefts)], refs[len(lefts) : -3], refs[-3]
        stacked, sems = refs[-2:]
        start = pl.multiple_of(lax.axis_index("dp") * depth, DH)
        own = pltpu.make_async_copy(g_ref.at[:, pl.ds(start, depth)], stacked.at[:rows], sems.at[pieces])
        own.start()
        copies = []
        for n in range(pieces):
            cut = pl.ds(n * height, height)
            copies.append(pltpu.make_async_copy(w_ref.at[cut], w_out.at[cut], sems.at[n]))
            copies[-1].start()
        for n, ref in enumerate(left_refs):
            stacked[(n + 1) * rows : (n + 2) * rows, :] = ref[...]
        own.wait()
        for n in range(pieces):
            cut = slice(n * height, (n + 1) * height)
            copies[n].wait()
            product = dot(stacked[...], w_out[cut, :], NT).astype(jnp.bfloat16)
            for out in range(count):
                outs[out][:, cut] = product[out * rows : (out + 1) * rows]

    shapes = (bf16(rows, total),) * count + (bf16(total, depth),)
    scratch = [pltpu.VMEM((count * rows, depth), jnp.bfloat16), pltpu.SemaphoreType.DMA((pieces + 1,))]
    operands = (Stays(grad_out), Stays(weight), *lefts)
    return call(body, shapes, operands, 2 * count * rows * depth * total, 4 * depth * total, scratch=scratch)


def gradient_product(left, weight, addends, span):
    blocks = left if isinstance(left, tuple) else (left,)
    height, depth = blocks[0].shape
    rows, width = height * len(blocks), span[1] - span[0]
    tile = 512 if width % 512 == 0 else width

    def body(*refs):
        w_ref = refs[len(blocks)]
        if len(blocks) > 1:
            for n in range(len(blocks)):
                at = pl.multiple_of((lax.axis_index("tensor") ^ n) * height, 16)
                refs[-1][pl.ds(at, height), :] = refs[n][...]
            whole, out = refs[-1], refs[-2]
        else:
            whole, out = refs[0], refs[-1]
        adds = refs[len(blocks) + 1 : len(blocks) + 1 + len(addends)]
        for start in range(0, width, tile):
            here = slice(span[0] + start, span[0] + start + tile)
            total = dot(whole[...], w_ref[here, :], NT)
            for ref in adds:
                total += ref[:, here].astype(jnp.float32)
            out[:, start : start + tile] = total.astype(jnp.bfloat16)

    cost = 2 * depth * width
    scratch = [pltpu.VMEM((rows, depth), jnp.bfloat16)] if len(blocks) > 1 else []
    return call(body, bf16(rows, width), (*blocks, weight, *addends), rows * cost, cost, scratch=scratch)


def output_products(layout, lefts, weight, near=(), halved=()):
    count, groups = len(lefts), len(lefts[0])
    rows = lefts[0][0].shape[0]
    depth, total = weight.shape
    width = layout.width
    tile = total // 2
    plain = [n for n in range(count) if n not in halved]
    results = len(near) + len(plain)
    stride = layout.fine // 2 if layout.halved else layout.fine

    def body(*refs):
        w_ref = refs[count * groups]
        near_refs = refs[count * groups + 1 : count * groups + 1 + len(near)]
        outs = refs[-1 - results - 2 * len(halved) : -1]
        stacked = refs[-1]
        for n in range(count):
            m = 0
            for group in range(groups):
                for part in range(lefts[n][group].shape[1] // width):
                    source = refs[n * groups + group][:, part * width : (part + 1) * width]
                    stacked[n * rows : (n + 1) * rows, layout.columns(m)] = source
                    m += 1
        for half in range(2):
            first = lax.axis_index("tensor") ^ half if halved else half
            cut = pl.ds(pl.multiple_of(first * tile, DH) if halved else first * tile, tile)
            product = dot(stacked[...], w_ref[:, cut], NN).astype(jnp.bfloat16)
            blocks = [ref[:, cut] for ref in near_refs] + [product[n * rows : (n + 1) * rows] for n in plain]
            for i in range(results):
                chosen = blocks[i]
                for other in range(stride, results if near else 0, stride):
                    swap = layout.swap() // (layout.fine // stride)
                    chosen = jnp.where(swap == other, blocks[i ^ other], chosen)
                outs[i][:, cut] = chosen
            for at, n in enumerate(halved):
                outs[results + 2 * at + half][...] = product[n * rows : (n + 1) * rows]

    operands = (*[part for left in lefts for part in left], weight, *near)
    scratch = [pltpu.VMEM((count * rows, depth), jnp.bfloat16)]
    shapes = (bf16(rows, total),) * results + (bf16(rows, tile),) * (2 * len(halved))
    cost = 2 * depth * total
    return call(body, shapes, operands, count * rows * cost, cost, scratch=scratch)


def joined(layout, pairs):
    rows, width = pairs[0][0].shape
    count = len(pairs)

    def body(*refs):
        totals = []
        for n in range(count):
            total = refs[2 * n][...].astype(jnp.float32) + refs[2 * n + 1][...].astype(jnp.float32)
            totals.append(total.astype(jnp.bfloat16))
        for i in range(count):
            chosen = totals[i]
            for other in range(1, count):
                chosen = jnp.where(layout.swap() // layout.fine == other, totals[i ^ other], chosen)
            refs[2 * count + i][...] = chosen

    size = rows * width * count
    return call(body, (bf16(rows, width),) * count, tuple(x for pair in pairs for x in pair), size, 6 * size)


def combined(layout, groups, halves):
    rows, width = groups[0][0].shape
    sizes = [len(group) for group in groups]
    half = width // 2
    at_end = list(halves)

    def body(*refs):
        out, sums, sems = refs[-3:]
        copies = []
        begin = sum(sizes)
        for n, i in enumerate(at_end):
            at = layout.place(i) * width + ((lax.axis_index("dp") ^ i) // layout.fine) * half
            there = out.at[:, pl.ds(pl.multiple_of(at, DH), half)]
            copies.append(pltpu.make_async_copy(refs[begin + n], there, sems.at[len(sizes) + n]))
            copies[-1].start()
        start = 0
        for f, size in enumerate(sizes):
            total = sum(ref[...].astype(jnp.float32) for ref in refs[start : start + size])
            start += size
            sums[f, :, :] = total.astype(jnp.bfloat16)
            at = pl.multiple_of(layout.place(f) * width, DH)
            copies.append(pltpu.make_async_copy(sums.at[f], out.at[:, pl.ds(at, width)], sems.at[f]))
            copies[-1].start()
        for copy in copies:
            copy.wait()

    size = rows * width * sum(sizes)
    operands = (*[part for group in groups for part in group], *[halves[i] for i in at_end])
    scratch = [
        pltpu.VMEM((len(sizes), rows, width), jnp.bfloat16),
        pltpu.SemaphoreType.DMA((len(sizes) + len(at_end),)),
    ]
    return call(body, bf16(rows, width * layout.fine), operands, size, 3 * size, scratch, 1)


def exchange(array, axis, mask):
    return lax.ppermute(array, axis, [(i, i ^ mask) for i in range(lax.axis_size(axis))])


def chain_sums(states, axis, reverse):
    devices = lax.axis_size(axis)
    links = [(i, i + 1) for i in range(devices - 1)]
    if reverse:
        links = [(devices - 1 - a, devices - 1 - b) for a, b in links]
    sums = []
    for state in states:
        total = None
        for link in links:
            arrived = lax.ppermute(state if total is None else state + total, axis, [link])
            total = arrived if total is None else total + arrived
        sums.append(total)
    return sums


def owned_sums(layout, states, axis, reverse):
    blocks = [states[0]]
    for m in range(1, len(states)):
        blocks.append(exchange(states[m], axis, m))
    sums = owner_sums(layout, blocks, reverse)
    result = [sums[0]]
    for m in range(1, len(states)):
        result.append(exchange(sums[m], axis, m))
    return result


def side_sums(layout, states, span, reverse):
    first, n = span[0] // DH, (span[1] - span[0]) // DH
    if layout.n_context != 4 or n % 2:
        return Sums(first, n, chain_sums([states], "context", reverse), reverse)
    neighbour = exchange(states, "context", 1)
    half = pair_half(states, neighbour)
    mine = exchange(half, "context", 2)
    other = exchange(mine, "context", 1)
    return Sums(first, n, [neighbour, mine, other], reverse)


def spans_of(heads, share):
    cut = int(heads * share) // 2 * 2
    return [(a * DH, b * DH) for a, b in ((0, cut), (cut, heads)) if a < b]


def shards(query_rows, key_rows, value_rows, out_weight, grad_out):
    seq_rows, head_width = query_rows.shape[1:]
    layout = Layout(head_width // DH)
    n_dp, n_tensor, parts = layout.n_dp, layout.n_tensor, layout.parts
    factor = float(DH * seq_rows * layout.n_context) ** (-0.5)
    piece = out_weight.shape[1]
    q, k, v = query_rows[0], key_rows[0], value_rows[0]
    bits = [1 << b for b in range(n_dp.bit_length() - 1)]
    top = bits[-1]
    everything = (0, head_width)
    far_spans = spans_of(head_width // DH, FAR_FIRST_SHARE)
    groups = 2 if parts % 2 == 0 else 1
    per = parts // groups

    halves = [mask for mask in range(top + 1, n_dp)] if n_tensor == 2 else []
    order = list(reversed(range(1, n_dp)))
    blocks = column_blocks(layout, grad_out[0], order, halves)
    taken = {}
    for mask, block in zip(order, blocks):
        taken[mask] = exchange(block, "dp", mask)
    for mask in halves:
        taken[mask] = (taken[mask], exchange(taken[mask], "tensor", 1))

    local_kv = key_value_states(layout, k, v)
    if layout.owned:
        prefix = owned_sums(layout, local_kv, "context", False)
    else:
        prefix = chain_sums(local_kv, "context", False)

    *products, weight = first_products(grad_out[0], [taken[m] for m in range(1, top)], out_weight)
    partial = dict(enumerate(products))

    def terms(mask, level):
        landed = []
        for b in range(level):
            part = added(mask | bits[b], b)
            landed.append(exchange(part, "dp", bits[b]))
        return landed

    def added(mask, level):
        landed = terms(mask, level)
        if mask not in partial:
            return gradient_product(taken[mask], weight, landed, everything)
        total = sum((x.astype(jnp.float32) for x in landed), partial[mask].astype(jnp.float32))
        return total.astype(jnp.bfloat16) if landed else partial[mask]

    kept = [partial[0], *terms(0, len(bits) - 1)]
    landed = terms(top, len(bits) - 1)
    grad, suffix = [], []
    for span in far_spans:
        far = gradient_product(taken[top], weight, landed, span)
        arrived = exchange(far, "dp", top)
        g, states = query_gradient_states(q, kept, arrived, span)
        grad.append(g)
        suffix.append(side_sums(layout, states, span, True))

    gathered = {0: []}
    for j in range(groups):
        gathered[0].append(attention(layout, q, k, v, prefix[j * per : (j + 1) * per], j * per, factor))
    for bit in reversed(bits):
        for mask in list(gathered):
            gathered[mask ^ bit] = []
            for j in range(groups):
                gathered[mask ^ bit].append(exchange(gathered[mask][j], "dp", bit))
    fine, coarse = layout.fine, layout.coarse
    part_width = piece // coarse
    close, distant = [gathered[m] for m in range(top)], [gathered[m] for m in range(top, n_dp)]
    if layout.halved:
        near, *halves_near = output_products(layout, close, weight, halved=(1,))
        whole = output_products(layout, distant[:1], weight, near=(near,))
        halves_rest = output_products(layout, distant[1:], weight, halved=(0,))
        pairs = []
        for (kept, sent) in (halves_near, halves_rest):
            pairs.append((kept, exchange(sent, "tensor", 1)))
        half = joined(layout, pairs)
        products = [whole[0], half[0], whole[1], half[1]]
    else:
        near = output_products(layout, close, weight)
        products = output_products(layout, distant, weight, near=near)
    landed, halves = [[] for _ in range(1 if layout.halved else fine)], {}
    for i in range(n_dp):
        for c in range(coarse):
            pairs = []
            for d in range(n_dp):
                for t in range(n_tensor):
                    s = ((t // coarse) * fine + d % fine) ^ i
                    to = (d // fine) * coarse + ((t % coarse) ^ c)
                    pairs.append((d * n_tensor + t, s * n_tensor + to))
            block = products[i]
            if coarse > 1:
                start = ((lax.axis_index("tensor") % coarse) ^ c) * part_width
                block = lax.dynamic_slice(block, (0, start), (seq_rows, part_width))
            block = lax.ppermute(block, ("dp", "tensor"), pairs)
            if layout.halved and i % 2:
                halves[i] = block
            else:
                landed[i % fine].append(block)
    attended = combined(layout, landed, halves)

    inside = []
    for j, span in enumerate(far_spans):
        inside.append(inside_gradients(q, k, v, grad[j], span))
    gq = query_gradients(grad, [x[0] for x in inside], [Listed(layout, prefix)], far_spans, factor)
    gkv = None
    for j, span in enumerate(far_spans):
        gkv = across_gradients(k, v, suffix[j : j + 1], *inside[j][1:], gkv, span, factor)
    return attended[None], gq[None], gkv[0][None], gkv[1][None]


def solution(mesh):
    rows = P("dp", "context", "tensor")
    in_specs = (rows, rows, rows, P("tensor", "dp"), P("dp", "context", None))

    return jax.shard_map(shards, mesh=mesh, in_specs=in_specs, out_specs=(rows,) * 4, check_vma=False)
```
